32 devices in a mesh: row: 4 (over z), col: 8 (over y, x, core).
Axes of the slice: x: 2, y: 2, z: 4, core: 2. Of those that a mesh axis runs over, the one named last changes fastest.
Arguments:
- root_factor: float32 [2, 4, 2560, 20480], P(None, 'row', None, 'col'), may hold values from -0.0390625 to 0.0390625
- root_rhs: float32 [20480, 64], P('col'), may hold values from -6 to 6
- child_factor: float32 [8, 4096, 4096], P('col', 'row'), may hold values from -0.09375 to 0.09375
- child_rhs: float32 [8, 4096, 64], P('col', 'row'), may hold values from -6 to 6
- child_map: int32 [8, 4096], P('col'), may hold values from 0 to 20479, as said below
Outputs:
- root_solution: float32 [20480, 64], P('col')
- child_solution: float32 [8, 4096, 64], P('col', 'row')
The draws below stay inside these ranges and needn't reach their ends.
Inputs may be any that keep to these rules, and one draw needn't show every extreme that they name: Each row of child_map is strictly increasing; its entries at positions j * 512 to (j + 1) * 512 - 1 lie in root rows j * 2560 to (j + 1) * 2560 - 1.
All inputs are finite; a program needn't handle non-finite values.
Results may differ from the reference program's by a relative error of at most 0.0001.
Values sent between devices are 32-bit elements; how exact they have to be, the bound alone decides.
No kernel may reach another device: no remote copies, remote signals or barrier semaphores. Data moves between devices by JAX's collectives and lax.ppermute only.
A program may use at most 128 MiB of HBM per device.

```python
import jax
import jax.numpy as jnp
from jax import lax

ROOT = 20480
PANEL = 2560
CP = 4096
CU = 4096
NRHS = 64
PANELS_ROW = 2
OWN_ROWS = 2560
PER_OWNER = 512
NFRONT = 8
N_ROW = 4


def draw_child_map(key, part):
    owners = ROOT // OWN_ROWS
    scores = jax.random.randint(key, (NFRONT, owners, OWN_ROWS), 0, 2 ** 19)
    places = jnp.arange(OWN_ROWS, dtype=jnp.int32)
    ends = (places == 0) | (places == OWN_ROWS - 1)
    forced = ends[None, None, :] & (jnp.arange(NFRONT, dtype=jnp.int32) == 0)[:, None, None]
    scores = jnp.where(forced, 2 ** 19, scores)
    distinct = scores * OWN_ROWS + places[None, None, :]
    chosen = lax.top_k(distinct, PER_OWNER)[1]
    chosen = jnp.sort(chosen, axis=-1)
    offsets = (jnp.arange(owners, dtype=jnp.int32) * OWN_ROWS)[None, :, None]
    return (chosen + offsets).reshape(NFRONT, CU).astype(jnp.int32)


def block_levels(key, dims, pieces, least, top_value):
    factor_of = 1.0
    for position, shards_of in pieces:
        heights = jax.random.uniform(jax.random.fold_in(jax.random.fold_in(key, 6), position), (shards_of,), jnp.float32, least / len(pieces), top_value / len(pieces))
        factor_of = factor_of * jnp.repeat(jnp.exp(heights), dims[position] // shards_of).reshape((-1,) + (1,) * (len(dims) - 1 - position))
    return factor_of


def bell_draw(own_key, extent, width, bound, cuts=(), kind=jnp.bfloat16):
    entries = jax.random.normal(own_key, extent, jnp.float32) * width
    if len(cuts) > 0:
        entries = block_levels(own_key, extent, cuts, -0.22, 0.18) * entries
    return jnp.clip(entries, min=-bound, max=bound).astype(kind)


def setup_inputs(seed: int = 0) -> dict:
    keys = jax.random.split(jax.random.key(seed), 6)
    root_factor = bell_draw(keys[0], (PANELS_ROW, N_ROW, PANEL, ROOT), ROOT ** -0.5, 0.0390625, ((1, 4), (3, 8)), jnp.float32)
    root_rhs = bell_draw(keys[1], (ROOT, NRHS), 1.0, 6.0, ((0, 8),), jnp.float32)
    child_factor = bell_draw(keys[2], (NFRONT, CP, CU), CU ** -0.5, 0.09375, ((0, 8), (1, 4)), jnp.float32)
    child_rhs = bell_draw(keys[3], (NFRONT, CP, NRHS), 1.0, 6.0, ((0, 8), (1, 4)), jnp.float32)
    child_map = draw_child_map(jax.random.fold_in(keys[5], 71), 0)
    return {"root_factor": root_factor, "root_rhs": root_rhs, "child_factor": child_factor, "child_rhs": child_rhs, "child_map": child_map}


def reference(root_factor, root_rhs, child_factor, child_rhs, child_map):
    factor_rows = root_factor.reshape(ROOT, ROOT)
    panels = ROOT // PANEL

    def advance(turn, solution):
        panel_id = (panels - 1 - turn) * PANEL
        panel_rows = lax.dynamic_slice_in_dim(factor_rows, panel_id, PANEL, 0)
        summed = jnp.dot(panel_rows, solution, precision=lax.Precision.HIGHEST, preferred_element_type=jnp.float32)
        update = lax.dynamic_slice_in_dim(root_rhs, panel_id, PANEL, 0) - summed
        return lax.dynamic_update_slice_in_dim(solution, update, panel_id, 0)

    root_solution = lax.fori_loop(0, panels, advance, jnp.zeros((ROOT, NRHS), jnp.float32))
    gathered = jnp.take(root_solution, child_map, axis=0)

    def apply_front(factor_pair):
        front_block, front_rows = factor_pair
        return jnp.dot(front_block, front_rows, precision=lax.Precision.HIGHEST, preferred_element_type=jnp.float32)

    child_solution = child_rhs - lax.map(apply_front, (child_factor, gathered))
    return root_solution, child_solution
```

```python
import functools

import jax
import jax.numpy as jnp
from jax import lax
from jax.experimental import pallas as pl
from jax.experimental.pallas import tpu as pltpu
from jax.sharding import PartitionSpec as P

F32 = jnp.float32
BF16 = jnp.bfloat16
ANY = pl.BlockSpec(memory_space=pl.ANY)
SMEM = pl.BlockSpec(memory_space=pltpu.SMEM)
NT = (((1,), (1,)), ((), ()))


def split(value):
    high = value.astype(BF16)
    return high, (value - high.astype(F32)).astype(BF16)


def aligned(index, size):
    return pl.ds(pl.multiple_of(index * size, size), size)


def chunk_of(rows):
    for size in (256, 128, 64, 32, 16, 8):
        if rows % size == 0:
            return size
    return rows


def stack_columns(x):
    high, low = split(x)
    both = jnp.concatenate([high.astype(F32), low.astype(F32)], axis=0)
    return both.T.astype(BF16)


def product(rows, stacked, count):
    high, low = split(rows)
    both = jnp.dot(high, stacked, preferred_element_type=F32)
    both += jnp.dot(low, stacked, preferred_element_type=F32)
    return (both[:, :count] + both[:, count:]).T


def update_kernel(step, pos, *refs):
    recvs = refs[: step["sources"]]
    rest = list(refs[step["sources"] :])
    carried = rest.pop(0) if step["carried"] else None
    rhs = rest.pop(0) if step["final"] else None
    factor, out, xbuf, tbuf, bbuf, stacked, lbuf, xsem, tsem, bsem, lsem, osem = rest
    row, col = pos[0], pos[1]
    slot, panel, n_row = step["slot"], step["panel"], step["n_row"]
    size = lbuf.shape[1]
    depth = lbuf.shape[0]
    chunks = out.shape[1] // size
    count = xbuf.shape[0]

    @pl.when((col == step["col"]) & (slot * n_row + row < panel))
    def _():
        def fetch(i, where):
            return pltpu.make_async_copy(
                factor.at[slot, 0, aligned(i, size)], lbuf.at[where], lsem.at[where]
            )

        def put(i):
            return pltpu.make_async_copy(
                tbuf.at[:, aligned(i, size)], out.at[:, aligned(i, size)], osem.at[i]
            )

        if step["sources"] == 1:
            pltpu.make_async_copy(recvs[0], xbuf, xsem).start()
        else:
            for d in range(n_row):

                @pl.when(lax.rem(panel - row + 2 * n_row, n_row) == d)
                def _():
                    pltpu.make_async_copy(recvs[d], xbuf, xsem).start()

        for i in range(min(depth - 1, chunks)):
            fetch(i, i).start()
        if carried is not None:
            pltpu.make_async_copy(carried, tbuf, tsem).start()
        pltpu.make_async_copy(recvs[0], xbuf, xsem).wait()
        stacked[...] = stack_columns(xbuf[...])
        if carried is not None:
            pltpu.make_async_copy(carried, tbuf, tsem).wait()
        else:
            tbuf[...] = jnp.zeros_like(tbuf)
        if rhs is not None:

            @pl.when(row == step["final_row"])
            def _():
                copy = pltpu.make_async_copy(rhs, bbuf, bsem)
                copy.start()
                copy.wait()
                tbuf[...] += bbuf[...]

        def advance(i, _):
            where = lax.rem(i, depth)
            fetch(i, where).wait()

            @pl.when(i + depth - 1 < chunks)
            def _():
                fetch(i + depth - 1, lax.rem(i + depth - 1, depth)).start()

            here = aligned(i, size)
            tbuf[:, here] = tbuf[:, here] - product(lbuf[where], stacked[...], count)
            put(i).start()
            return 0

        lax.fori_loop(0, chunks, advance, 0)

        def finish(i, _):
            put(i).wait()
            return 0

        lax.fori_loop(0, chunks, finish, 0)


def update(step, pos, recvs, carried, rhs, factor):
    panel_rows, own = factor.shape[2], factor.shape[3]
    count = recvs[0].shape[0]
    size = chunk_of(panel_rows)
    depth = 4
    operands = [*recvs]
    if carried is not None:
        operands.append(carried)
    if rhs is not None:
        operands.append(rhs)
    operands.append(factor)
    return pl.pallas_call(
        functools.partial(update_kernel, step),
        out_shape=jax.ShapeDtypeStruct((count, panel_rows), F32),
        in_specs=[SMEM] + [ANY] * len(operands),
        out_specs=ANY,
        scratch_shapes=[
            pltpu.VMEM((count, own), F32),
            pltpu.VMEM((count, panel_rows), F32),
            pltpu.VMEM((count, panel_rows), F32),
            pltpu.VMEM((own, 2 * count), BF16),
            pltpu.VMEM((depth, size, own), F32),
            pltpu.SemaphoreType.DMA,
            pltpu.SemaphoreType.DMA,
            pltpu.SemaphoreType.DMA,
            pltpu.SemaphoreType.DMA((depth,)),
            pltpu.SemaphoreType.DMA((panel_rows // size,)),
        ],
        compiler_params=pltpu.CompilerParams(vmem_limit_bytes=28 << 20),
        cost_estimate=pl.CostEstimate(
            flops=4 * 2 * panel_rows * own * count,
            bytes_accessed=4 * panel_rows * own,
            transcendentals=0,
        ),
        name=f"update_{step['col']}_{step['slot']}",
    )(pos, *operands)


def serve_kernel(cases, pos, wanted, *refs):
    sources = refs[: len(cases)]
    own_out, out, xbuf, stacked, gbuf, xsem, ysem, gsem = refs[len(cases) :]
    row, col = pos[0], pos[1]
    count, own = xbuf.shape
    fronts, per = wanted.shape
    for case, source in zip(cases, sources):
        want_col, distance, panel, n_row = case
        chosen = col == want_col
        if distance is not None:
            chosen &= lax.rem(panel - row + 2 * n_row, n_row) == distance

        @pl.when(chosen)
        def _():
            pltpu.make_async_copy(source, xbuf, xsem).start()

    pltpu.make_async_copy(sources[0], xbuf, xsem).wait()
    keep = pltpu.make_async_copy(xbuf, own_out, ysem)
    keep.start()
    high, low = split(xbuf[...])
    stacked[:count, :] = high
    stacked[count:, :] = low
    tile = chunk_of(own)

    def gather(f, _):
        index = wanted[pl.ds(f, 1), :]
        total = jnp.zeros((2 * count, per), F32)
        for t in range(own // tile):
            places = lax.broadcasted_iota(jnp.int32, (tile, per), 0) + t * tile
            hot = jnp.where(places == index, 1.0, 0.0).astype(BF16)
            total += jnp.dot(
                stacked[:, t * tile : (t + 1) * tile], hot, preferred_element_type=F32
            )
        gbuf[f] = total[:count] + total[count:]
        pltpu.make_async_copy(gbuf.at[f], out.at[f], gsem.at[f]).start()
        return 0

    lax.fori_loop(0, fronts, gather, 0)

    def finish(f, _):
        pltpu.make_async_copy(gbuf.at[f], out.at[f], gsem.at[f]).wait()
        return 0

    lax.fori_loop(0, fronts, finish, 0)
    keep.wait()


def serve(cases, pos, wanted, sources):
    count, own = sources[0].shape
    fronts, per = wanted.shape
    return pl.pallas_call(
        functools.partial(serve_kernel, cases),
        out_shape=(
            jax.ShapeDtypeStruct((count, own), F32),
            jax.ShapeDtypeStruct((fronts, count, per), F32),
        ),
        in_specs=[SMEM, pl.BlockSpec(memory_space=pltpu.VMEM)] + [ANY] * len(sources),
        out_specs=(ANY, ANY),
        scratch_shapes=[
            pltpu.VMEM((count, own), F32),
            pltpu.VMEM((2 * count, own), BF16),
            pltpu.VMEM((fronts, count, per), F32),
            pltpu.SemaphoreType.DMA,
            pltpu.SemaphoreType.DMA,
            pltpu.SemaphoreType.DMA((fronts,)),
        ],
        compiler_params=pltpu.CompilerParams(vmem_limit_bytes=24 << 20),
        name="serve",
    )(pos, wanted, *sources)


def couple_kernel(parents, factor, rhs, out, stacked, lbuf, lsem):
    count = rhs.shape[0]
    fronts, per = parents.shape[0], parents.shape[2]
    size, depth = lbuf.shape[1], lbuf.shape[0]
    chunks = out.shape[1] // size

    def fetch(i, where):
        return pltpu.make_async_copy(
            factor.at[aligned(i, size)], lbuf.at[where], lsem.at[where]
        )

    for i in range(min(depth - 1, chunks)):
        fetch(i, i).start()
    for f in range(fronts):
        stacked[f * per : (f + 1) * per, :] = stack_columns(parents[f])

    def advance(i, _):
        where = lax.rem(i, depth)
        fetch(i, where).wait()

        @pl.when(i + depth - 1 < chunks)
        def _():
            fetch(i + depth - 1, lax.rem(i + depth - 1, depth)).start()

        here = aligned(i, size)
        out[:, here] = rhs[:, here] - product(lbuf[where], stacked[...], count)
        return 0

    lax.fori_loop(0, chunks, advance, 0)


def couple(parents, factor, rhs):
    rows, updates = factor.shape
    count = rhs.shape[0]
    size = chunk_of(rows // 2)
    vmem = pl.BlockSpec(memory_space=pltpu.VMEM)
    depth = 3
    return pl.pallas_call(
        couple_kernel,
        out_shape=jax.ShapeDtypeStruct((count, rows), F32),
        in_specs=[vmem, ANY, vmem],
        out_specs=vmem,
        scratch_shapes=[
            pltpu.VMEM((updates, 2 * count), BF16),
            pltpu.VMEM((depth, size, updates), F32),
            pltpu.SemaphoreType.DMA((depth,)),
        ],
        compiler_params=pltpu.CompilerParams(vmem_limit_bytes=40 << 20),
        name="couple",
    )(parents, factor, rhs)


def body(root_factor, root_rhs, child_factor, child_rhs, child_map):
    n_row, n_col = lax.axis_size("row"), lax.axis_size("col")
    slots, panel_rows, own = root_factor.shape[0], root_factor.shape[2], root_factor.shape[3]
    panels = slots * n_row
    pieces = n_col // panels
    row, col = lax.axis_index("row"), lax.axis_index("col")
    pos = jnp.stack([row, col]).astype(jnp.int32)
    per_front = child_map.shape[1] // n_col

    def move(value, pairs):
        flat = [(a * n_col + b, c * n_col + d) for (a, b), (c, d) in pairs]
        return lax.ppermute(value, ("row", "col"), flat)

    asked = lax.all_to_all(
        child_map.reshape(n_col, per_front), "col", split_axis=0, concat_axis=0, tiled=True
    )
    asked = asked - col * own
    own_rhs = root_rhs.T
    ahead = [
        move(
            own_rhs,
            [
                ((k % n_row, k * pieces + i), (k % n_row, (k + 1) * pieces))
                for k in range(panels - 1)
            ],
        )
        for i in range(pieces)
    ]
    ahead = ahead[0] if pieces == 1 else jnp.concatenate(ahead, axis=1)

    arrived = {c: [own_rhs] for c in range((panels - 1) * pieces, n_col)}
    carried = [None] * slots
    for c in range(n_col - 1, pieces - 1, -1):
        panel = c // pieces
        final = panel - 1 if c % pieces == 0 else None
        for slot in range(slots - 1, -1, -1):
            active = [r for r in range(n_row) if slot * n_row + r < panel]
            if not active:
                continue
            ends = final is not None and final // n_row == slot
            step = {
                "col": c,
                "slot": slot,
                "panel": panel,
                "n_row": n_row,
                "sources": len(arrived[c]),
                "carried": carried[slot] is not None,
                "final": ends,
                "final_row": final % n_row if ends else None,
            }
            out = update(
                step, pos, arrived[c], carried[slot], ahead if ends else None, root_factor
            )
            if ends:
                source = final % n_row
                order = [*range(1, n_row), 0]
                for i in range(pieces):
                    piece = out[:, i * own : (i + 1) * own] if pieces > 1 else out
                    target = final * pieces + i
                    got = {
                        d: move(piece, [((source, c), ((source - d) % n_row, target))])
                        for d in order
                    }
                    arrived[target] = [got[d] for d in range(n_row)]
                active.remove(source)
            if active:
                carried[slot] = move(out, [((r, c), (r, c - 1)) for r in active])

    cases, sources = [], []
    for c in range(n_col):
        if len(arrived[c]) == 1:
            cases.append((c, None, None, n_row))
            sources.append(arrived[c][0])
        else:
            for d in range(n_row):
                cases.append((c, d, c // pieces, n_row))
                sources.append(arrived[c][d])
    solved, served = serve(tuple(cases), pos, asked, sources)
    parents = lax.all_to_all(served, "col", split_axis=0, concat_axis=0, tiled=True)
    child = couple(parents, child_factor[0], child_rhs[0].T)
    return solved.T, child.T[None]


def solution(mesh):
    return jax.shard_map(
        body,
        mesh=mesh,
        in_specs=(
            P(None, "row", None, "col"),
            P("col", None),
            P("col", "row", None),
            P("col", "row", None),
            P("col", None),
        ),
        out_specs=(P("col", None), P("col", "row", None)),
        check_vma=False,
    )
```

```python
import functools

import jax
import jax.numpy as jnp
from jax import lax
from jax.experimental import pallas as pl
from jax.experimental.pallas import tpu as pltpu
from jax.sharding import PartitionSpec as P


F32 = jnp.float32
BF16 = jnp.bfloat16
ANY = pl.BlockSpec(memory_space=pl.ANY)
SMEM = pl.BlockSpec(memory_space=pltpu.SMEM)


def split(value):
    high = value.astype(BF16)
    return high, (value - high.astype(F32)).astype(BF16)


def aligned(index, size):
    return pl.ds(pl.multiple_of(index * size, size), size)


def chunk_of(rows):
    for size in (256, 128, 64, 32, 16, 8):
        if rows % size == 0:
            return size
    return rows


def stack_columns(x):
    high, low = split(x)
    both = jnp.concatenate([high.astype(F32), low.astype(F32)], axis=0)
    return both.T.astype(BF16)


def product(rows, stacked, count):
    high, low = split(rows)
    both = jnp.dot(high, stacked, preferred_element_type=F32)
    both += jnp.dot(low, stacked, preferred_element_type=F32)
    return (both[:, :count] + both[:, count:]).T


def update_kernel(step, pos, *refs):
    recvs = refs[: step["sources"]]
    rest = list(refs[step["sources"] :])
    carried = rest.pop(0) if step["carried"] else None
    rhs = rest.pop(0) if step["final"] else None
    factor, out, xbuf, tbuf, bbuf, stacked, lbuf, xsem, tsem, bsem, lsem, osem = rest
    row, col = pos[0], pos[1]
    slot, panel, n_row = step["slot"], step["panel"], step["n_row"]
    size = lbuf.shape[1]
    depth = lbuf.shape[0]
    chunks = out.shape[1] // size
    count = xbuf.shape[0]

    @pl.when((col == step["col"]) & (slot * n_row + row < panel))
    def _():
        def fetch(i, where):
            return pltpu.make_async_copy(
                factor.at[slot, 0, aligned(i, size)], lbuf.at[where], lsem.at[where]
            )

        def put(i):
            return pltpu.make_async_copy(
                tbuf.at[:, aligned(i, size)], out.at[:, aligned(i, size)], osem.at[i]
            )

        if step["sources"] == 1:
            pltpu.make_async_copy(recvs[0], xbuf, xsem).start()
        else:
            for d in range(n_row):

                @pl.when(lax.rem(panel - row + 2 * n_row, n_row) == d)
                def _():
                    pltpu.make_async_copy(recvs[d], xbuf, xsem).start()

        for i in range(min(depth - 1, chunks)):
            fetch(i, i).start()
        if carried is not None:
            pltpu.make_async_copy(carried, tbuf, tsem).start()
        pltpu.make_async_copy(recvs[0], xbuf, xsem).wait()
        stacked[...] = stack_columns(xbuf[...])
        if carried is not None:
            pltpu.make_async_copy(carried, tbuf, tsem).wait()
        else:
            tbuf[...] = jnp.zeros_like(tbuf)
        if rhs is not None:

            @pl.when(row == step["final_row"])
            def _():
                copy = pltpu.make_async_copy(rhs, bbuf, bsem)
                copy.start()
                copy.wait()
                tbuf[...] += bbuf[...]

        def advance(i, _):
            where = lax.rem(i, depth)
            fetch(i, where).wait()

            @pl.when(i + depth - 1 < chunks)
            def _():
                fetch(i + depth - 1, lax.rem(i + depth - 1, depth)).start()

            here = aligned(i, size)
            tbuf[:, here] = tbuf[:, here] - product(lbuf[where], stacked[...], count)
            put(i).start()
            return 0

        lax.fori_loop(0, chunks, advance, 0)

        def finish(i, _):
            put(i).wait()
            return 0

        lax.fori_loop(0, chunks, finish, 0)


def update(step, pos, recvs, carried, rhs, factor):
    panel_rows, own = factor.shape[2], factor.shape[3]
    count = recvs[0].shape[0]
    size = chunk_of(panel_rows)
    depth = 4
    operands = [*recvs]
    if carried is not None:
        operands.append(carried)
    if rhs is not None:
        operands.append(rhs)
    operands.append(factor)
    return pl.pallas_call(
        functools.partial(update_kernel, step),
        out_shape=jax.ShapeDtypeStruct((count, panel_rows), F32),
        in_specs=[SMEM] + [ANY] * len(operands),
        out_specs=ANY,
        scratch_shapes=[
            pltpu.VMEM((count, own), F32),
            pltpu.VMEM((count, panel_rows), F32),
            pltpu.VMEM((count, panel_rows), F32),
            pltpu.VMEM((own, 2 * count), BF16),
            pltpu.VMEM((depth, size, own), F32),
            pltpu.SemaphoreType.DMA,
            pltpu.SemaphoreType.DMA,
            pltpu.SemaphoreType.DMA,
            pltpu.SemaphoreType.DMA((depth,)),
            pltpu.SemaphoreType.DMA((panel_rows // size,)),
        ],
        compiler_params=pltpu.CompilerParams(vmem_limit_bytes=28 << 20),
        cost_estimate=pl.CostEstimate(
            flops=4 * 2 * panel_rows * own * count,
            bytes_accessed=4 * panel_rows * own,
            transcendentals=0,
        ),
    )(pos, *operands)


def serve_kernel(cases, pos, wanted, *refs):
    sources = refs[: len(cases)]
    own_out, out, xbuf, stacked, gbuf, xsem, ysem, gsem = refs[len(cases) :]
    row, col = pos[0], pos[1]
    count, own = xbuf.shape
    fronts, per = wanted.shape
    for case, source in zip(cases, sources):
        want_col, distance, panel, n_row = case
        chosen = col == want_col
        if distance is not None:
            chosen &= lax.rem(panel - row + 2 * n_row, n_row) == distance

        @pl.when(chosen)
        def _():
            pltpu.make_async_copy(source, xbuf, xsem).start()

    pltpu.make_async_copy(sources[0], xbuf, xsem).wait()
    keep = pltpu.make_async_copy(xbuf, own_out, ysem)
    keep.start()
    high, low = split(xbuf[...])
    stacked[:count, :] = high
    stacked[count:, :] = low
    tile = chunk_of(own)

    def gather(f, _):
        index = wanted[pl.ds(f, 1), :]
        total = jnp.zeros((2 * count, per), F32)
        for t in range(own // tile):
            places = lax.broadcasted_iota(jnp.int32, (tile, per), 0) + t * tile
            hot = jnp.where(places == index, 1.0, 0.0).astype(BF16)
            total += jnp.dot(
                stacked[:, t * tile : (t + 1) * tile], hot, preferred_element_type=F32
            )
        gbuf[f] = total[:count] + total[count:]
        pltpu.make_async_copy(gbuf.at[f], out.at[f], gsem.at[f]).start()
        return 0

    lax.fori_loop(0, fronts, gather, 0)

    def finish(f, _):
        pltpu.make_async_copy(gbuf.at[f], out.at[f], gsem.at[f]).wait()
        return 0

    lax.fori_loop(0, fronts, finish, 0)
    keep.wait()


def serve(cases, pos, wanted, sources):
    count, own = sources[0].shape
    fronts, per = wanted.shape
    return pl.pallas_call(
        functools.partial(serve_kernel, cases),
        out_shape=(
            jax.ShapeDtypeStruct((count, own), F32),
            jax.ShapeDtypeStruct((fronts, count, per), F32),
        ),
        in_specs=[SMEM, pl.BlockSpec(memory_space=pltpu.VMEM)] + [ANY] * len(sources),
        out_specs=(ANY, ANY),
        scratch_shapes=[
            pltpu.VMEM((count, own), F32),
            pltpu.VMEM((2 * count, own), BF16),
            pltpu.VMEM((fronts, count, per), F32),
            pltpu.SemaphoreType.DMA,
            pltpu.SemaphoreType.DMA,
            pltpu.SemaphoreType.DMA((fronts,)),
        ],
        compiler_params=pltpu.CompilerParams(vmem_limit_bytes=24 << 20),
        name="serve",
    )(pos, wanted, *sources)


def couple_kernel(parents, factor, rhs, out, stacked, lbuf, lsem):
    count = rhs.shape[0]
    fronts, per = parents.shape[0], parents.shape[2]
    size, depth = lbuf.shape[1], lbuf.shape[0]
    chunks = out.shape[1] // size

    def fetch(i, where):
        return pltpu.make_async_copy(
            factor.at[aligned(i, size)], lbuf.at[where], lsem.at[where]
        )

    for i in range(min(depth - 1, chunks)):
        fetch(i, i).start()
    for f in range(fronts):
        stacked[f * per : (f + 1) * per, :] = stack_columns(parents[f])

    def advance(i, _):
        where = lax.rem(i, depth)
        fetch(i, where).wait()

        @pl.when(i + depth - 1 < chunks)
        def _():
            fetch(i + depth - 1, lax.rem(i + depth - 1, depth)).start()

        here = aligned(i, size)
        out[:, here] = rhs[:, here] - product(lbuf[where], stacked[...], count)
        return 0

    lax.fori_loop(0, chunks, advance, 0)


def couple(parents, factor, rhs):
    rows, updates = factor.shape
    count = rhs.shape[0]
    size = chunk_of(rows // 2)
    vmem = pl.BlockSpec(memory_space=pltpu.VMEM)
    depth = 3
    return pl.pallas_call(
        couple_kernel,
        out_shape=jax.ShapeDtypeStruct((count, rows), F32),
        in_specs=[vmem, ANY, vmem],
        out_specs=vmem,
        scratch_shapes=[
            pltpu.VMEM((updates, 2 * count), BF16),
            pltpu.VMEM((depth, size, updates), F32),
            pltpu.SemaphoreType.DMA((depth,)),
        ],
        compiler_params=pltpu.CompilerParams(vmem_limit_bytes=40 << 20),
        name="couple",
    )(parents, factor, rhs)


def plain_body(root_factor, root_rhs, child_factor, child_rhs, child_map):
    n_row, n_col = lax.axis_size("row"), lax.axis_size("col")
    slots, own = root_factor.shape[0], root_factor.shape[3]
    panels = slots * n_row
    pieces = n_col // panels
    row, col = lax.axis_index("row"), lax.axis_index("col")
    pos = jnp.stack([row, col]).astype(jnp.int32)
    per_front = child_map.shape[1] // n_col

    def move(value, pairs):
        flat = [(a * n_col + b, c * n_col + d) for (a, b), (c, d) in pairs]
        return lax.ppermute(value, ("row", "col"), flat)

    asked = lax.all_to_all(
        child_map.reshape(n_col, per_front), "col", split_axis=0, concat_axis=0, tiled=True
    )
    asked = asked - col * own
    own_rhs = root_rhs.T
    ahead = [
        move(
            own_rhs,
            [
                ((k % n_row, k * pieces + i), (k % n_row, (k + 1) * pieces))
                for k in range(panels - 1)
            ],
        )
        for i in range(pieces)
    ]
    ahead = ahead[0] if pieces == 1 else jnp.concatenate(ahead, axis=1)

    arrived = {c: [own_rhs] for c in range((panels - 1) * pieces, n_col)}
    carried = [None] * slots
    for c in range(n_col - 1, pieces - 1, -1):
        panel = c // pieces
        final = panel - 1 if c % pieces == 0 else None
        for slot in range(slots - 1, -1, -1):
            active = [r for r in range(n_row) if slot * n_row + r < panel]
            if not active:
                continue
            ends = final is not None and final // n_row == slot
            step = {
                "col": c,
                "slot": slot,
                "panel": panel,
                "n_row": n_row,
                "sources": len(arrived[c]),
                "carried": carried[slot] is not None,
                "final": ends,
                "final_row": final % n_row if ends else None,
            }
            out = update(
                step, pos, arrived[c], carried[slot], ahead if ends else None, root_factor
            )
            if ends:
                source = final % n_row
                order = [*range(1, n_row), 0]
                for i in range(pieces):
                    piece = out[:, i * own : (i + 1) * own] if pieces > 1 else out
                    target = final * pieces + i
                    got = {
                        d: move(piece, [((source, c), ((source - d) % n_row, target))])
                        for d in order
                    }
                    arrived[target] = [got[d] for d in range(n_row)]
                active.remove(source)
            if active:
                carried[slot] = move(out, [((r, c), (r, c - 1)) for r in active])

    cases, sources = [], []
    for c in range(n_col):
        if len(arrived[c]) == 1:
            cases.append((c, None, None, n_row))
            sources.append(arrived[c][0])
        else:
            for d in range(n_row):
                cases.append((c, d, c // pieces, n_row))
                sources.append(arrived[c][d])
    solved, served = serve(tuple(cases), pos, asked, sources)
    parents = lax.all_to_all(served, "col", split_axis=0, concat_axis=0, tiled=True)
    child = couple(parents, child_factor[0], child_rhs[0].T)
    return solved.T, child.T[None]


def block_kernel(plan, pos, *refs):
    refs = list(refs)
    sources = [[refs.pop(0) for _ in parts] for _, parts in plan["sources"]]
    rhs = refs.pop(0)
    bases = [refs.pop(0) for _ in plan["bases"]]
    before = refs.pop(0) if plan["whole"] else None
    factor = refs.pop(0)
    del refs[: plan["waits"]]
    out = refs.pop(0)
    whole = refs.pop(0) if plan["whole"] else None
    xbuf, bbuf, tbuf, ubuf, pbuf, stacked, lbuf, xsem, bsem, tsem, lsem, osem, wsem = refs
    row, col = pos[0], pos[1]
    depth, size, width = lbuf.shape
    first_row, first_column = plan["first_row"], plan["first_column"]
    count, rows = tbuf.shape
    chunks = rows // size
    active = (col == plan["col"]) & (plan["slot"] * plan["n_row"] + row < plan["col"])
    if plan["only"] is not None:
        active &= row == plan["only"]
    if plan["without"] is not None:
        active &= row != plan["without"]

    @pl.when(active)
    def _():
        def fetch(i, where):
            return pltpu.make_async_copy(
                factor.at[
                    plan["slot"],
                    0,
                    pl.ds(pl.multiple_of(first_row + i * size, size), size),
                    pl.ds(first_column, width),
                ],
                lbuf.at[where],
                lsem.at[where],
            )

        def put(i):
            return pltpu.make_async_copy(
                tbuf.at[:, aligned(i, size)], out.at[:, aligned(i, size)], osem.at[i]
            )

        def put_whole(i):
            return pltpu.make_async_copy(
                tbuf.at[:, aligned(i, size)],
                whole.at[:, pl.ds(pl.multiple_of(first_row + i * size, size), size)],
                wsem.at[i],
            )

        def take(parts, ends):
            copies = []
            for n, (ref, (source_at, at, size_of)) in enumerate(zip(parts, ends)):
                copies.append(
                    pltpu.make_async_copy(
                        ref.at[:, pl.ds(source_at, size_of)],
                        xbuf.at[:, pl.ds(at, size_of)],
                        xsem.at[n],
                    )
                )
            for copy in copies:
                copy.start()
            for copy in copies:
                copy.wait()

        load_rhs = pltpu.make_async_copy(rhs.at[:, pl.ds(first_column, width)], bbuf, bsem)
        load_rhs.start()
        for i in range(min(depth - 1, chunks)):
            fetch(i, i).start()
        loads = []
        for n, (ref, at) in enumerate(zip(bases, plan["bases"])):
            where = (tbuf, ubuf)[n]
            loads.append(pltpu.make_async_copy(ref.at[:, pl.ds(at, rows)], where, tsem.at[n]))
            loads[-1].start()
        if before is not None:
            load_before = pltpu.make_async_copy(before, pbuf, wsem.at[chunks])
            load_before.start()
        for (distance, ends), parts in zip(plan["sources"], sources):
            if distance is None:
                take(parts, ends)
            else:

                @pl.when(lax.rem(plan["col"] - row + 2 * plan["n_row"], plan["n_row"]) == distance)
                def _():
                    take(parts, ends)

        load_rhs.wait()
        x = bbuf[...] + xbuf[...] if sources else bbuf[...]
        bbuf[...] = x

        def fill(i, _):
            stacked[aligned(i, chunk_of(width)), :] = stack_columns(
                bbuf[:, aligned(i, chunk_of(width))]
            )
            return 0

        lax.fori_loop(0, width // chunk_of(width), fill, 0)
        for copy in loads:
            copy.wait()
        if not bases:
            tbuf[...] = jnp.zeros_like(tbuf)
        if len(bases) == 2:
            tbuf[...] += ubuf[...]
        if before is not None:
            load_before.wait()
            put_before = pltpu.make_async_copy(
                pbuf, whole.at[:, pl.ds(0, first_row)], wsem.at[chunks]
            )
            put_before.start()

        def advance(i, _):
            where = lax.rem(i, depth)
            fetch(i, where).wait()

            @pl.when(i + depth - 1 < chunks)
            def _():
                fetch(i + depth - 1, lax.rem(i + depth - 1, depth)).start()

            here = aligned(i, size)
            tbuf[:, here] = tbuf[:, here] - product(lbuf[where], stacked[...], count)
            put(i).start()
            if whole is not None:
                put_whole(i).start()
            return 0

        lax.fori_loop(0, chunks, advance, 0)

        def finish(i, _):
            put(i).wait()
            if whole is not None:
                put_whole(i).wait()
            return 0

        lax.fori_loop(0, chunks, finish, 0)
        if before is not None:
            put_before.wait()


def block(
    pos, factor, rhs, *, col, slot, rows, columns, sources=(), bases=(), before=None,
    whole_over=None, only=None, without=None, waits=(),
):
    n_row = lax.axis_size("row")
    count = rhs.shape[0]
    first_row, high = rows
    first_column, width = columns
    size = chunk_of(high) if only is not None else chunk_of(high) // 2
    depth = 4 if only is not None else 8
    plan = {
        "sources": [(d, tuple(p[1:] for p in parts)) for d, parts in sources],
        "bases": [at for _, at in bases],
        "whole": before is not None,
        "waits": len(waits) + (whole_over is not None),
        "first_row": first_row,
        "first_column": first_column,
        "col": col,
        "slot": slot,
        "n_row": n_row,
        "only": only,
        "without": without,
    }
    operands = [p[0] for _, parts in sources for p in parts]
    operands += [rhs] + [array for array, _ in bases]
    if before is not None:
        operands.append(before)
    operands.append(factor)
    operands += list(waits)
    aliases = {}
    shapes = [jax.ShapeDtypeStruct((count, high), F32)]
    if before is not None:
        aliases = {len(operands) + 1: 1}
        operands.append(whole_over)
        shapes.append(jax.ShapeDtypeStruct(whole_over.shape, F32))
    chunks = high // size
    got = pl.pallas_call(
        functools.partial(block_kernel, plan),
        out_shape=tuple(shapes),
        in_specs=[SMEM] + [ANY] * len(operands),
        out_specs=(ANY,) * len(shapes),
        input_output_aliases=aliases,
        scratch_shapes=[
            pltpu.VMEM((count, width), F32),
            pltpu.VMEM((count, width), F32),
            pltpu.VMEM((count, high), F32),
            pltpu.VMEM((count, high), F32),
            pltpu.VMEM((count, max(first_row, 128)), F32),
            pltpu.VMEM((width, 2 * count), BF16),
            pltpu.VMEM((depth, size, width), F32),
            pltpu.SemaphoreType.DMA((2,)),
            pltpu.SemaphoreType.DMA,
            pltpu.SemaphoreType.DMA((2,)),
            pltpu.SemaphoreType.DMA((depth,)),
            pltpu.SemaphoreType.DMA((chunks,)),
            pltpu.SemaphoreType.DMA((chunks + 1,)),
        ],
        compiler_params=pltpu.CompilerParams(vmem_limit_bytes=24 << 20),
        cost_estimate=pl.CostEstimate(
            flops=8 * high * width * count,
            bytes_accessed=4 * high * width,
            transcendentals=0,
        ),
    )(pos, *operands)
    return got if before is not None else got[0]


def choose(row, panel, n_row, sources, rhs, xbuf, bbuf, xsem, bsem):
    load = pltpu.make_async_copy(rhs, bbuf, bsem)
    load.start()
    for distance, parts in sources:

        @pl.when(lax.rem(panel - row + 2 * n_row, n_row) == distance)
        def _():
            copies = [
                pltpu.make_async_copy(
                    ref.at[:, pl.ds(source_at, size)], xbuf.at[:, pl.ds(at, size)], xsem.at[n]
                )
                for n, (ref, source_at, at, size) in enumerate(parts)
            ]
            for copy in copies:
                copy.start()
            for copy in copies:
                copy.wait()

    load.wait()
    bbuf[...] += xbuf[...]


def keep_kernel(plan, pos, *refs):
    refs = list(refs)
    sources = [
        (d, [(refs.pop(0), *ends) for ends in parts]) for d, parts in plan["sources"]
    ]
    rhs = refs.pop(0)
    refs = refs[plan["waits"] :]
    out, xbuf, bbuf, xsem, bsem = refs

    @pl.when(pos[1] == plan["col"])
    def _():
        choose(pos[0], plan["col"], plan["n_row"], sources, rhs, xbuf, bbuf, xsem, bsem)
        copy = pltpu.make_async_copy(bbuf, out, bsem)
        copy.start()
        copy.wait()


def keep(pos, col, sources, rhs, over, waits):
    plan = {
        "col": col,
        "n_row": lax.axis_size("row"),
        "sources": [(d, tuple(p[1:] for p in parts)) for d, parts in sources],
        "waits": len(waits) + (over is not None),
    }
    operands = [p[0] for _, parts in sources for p in parts] + [rhs, *waits]
    aliases = {}
    if over is not None:
        aliases = {len(operands) + 1: 0}
        operands.append(over)
    return pl.pallas_call(
        functools.partial(keep_kernel, plan),
        out_shape=jax.ShapeDtypeStruct(rhs.shape, F32),
        in_specs=[SMEM] + [ANY] * len(operands),
        out_specs=ANY,
        input_output_aliases=aliases,
        scratch_shapes=[
            pltpu.VMEM(rhs.shape, F32),
            pltpu.VMEM(rhs.shape, F32),
            pltpu.SemaphoreType.DMA((2,)),
            pltpu.SemaphoreType.DMA,
        ],
        compiler_params=pltpu.CompilerParams(vmem_limit_bytes=4 << 20),
    )(pos, *operands)


def chain_body(root_factor, root_rhs, child_factor, child_rhs, child_map):
    n_row, n_col = lax.axis_size("row"), lax.axis_size("col")
    own = root_factor.shape[3]
    half = own // 2
    row, col = lax.axis_index("row"), lax.axis_index("col")
    pos = jnp.stack([row, col]).astype(jnp.int32)
    per_front = child_map.shape[1] // n_col
    rhs = root_rhs.T

    def move(value, pairs):
        flat = [(a * n_col + b, c * n_col + d) for (a, b), (c, d) in pairs]
        return lax.ppermute(value, ("row", "col"), flat)

    early = late = None
    others = {}
    shifted = {}
    solved = None
    asked = None
    for c in range(n_col - 1, 0, -1):
        target = (c - 1) % n_row
        ends = (c - 1) // n_row
        last = c == n_col - 1
        came = c // n_row
        sources = []
        if not last:
            sources.append((0, ((shifted[came], 0, 0, own),)))
            sources.append((1, ((early, 0, 0, half), (late, 0, half, half))))
            sources += [(d, ((others[d], 0, 0, own),)) for d in range(2, n_row)]
        base = [] if last else [(shifted[ends], 0)]
        total = block(
            pos, root_factor, rhs, col=c, slot=ends, rows=(0, own),
            columns=(0, half), sources=[] if last else [(None, ((early, 0, 0, half),))],
            only=target,
        )
        upper_x = [] if last else [(None, ((late, 0, 0, half),))]
        upper = block(
            pos, root_factor, rhs, col=c, slot=ends, rows=(0, half),
            columns=(half, half), sources=upper_x, only=target,
            bases=[(total, 0)] + [(a, 0) for a, _ in base],
        )
        beside = block(
            pos, root_factor, rhs, col=c, slot=ends, rows=(0, own),
            columns=(0, own), sources=sources, bases=base, without=target, waits=(upper,),
        )
        lower, whole = block(
            pos, root_factor, rhs, col=c, slot=ends, rows=(half, half),
            columns=(half, half), sources=upper_x, only=target,
            bases=[(total, half)] + [(a, half) for a, _ in base],
            before=upper, whole_over=beside,
        )
        pair = [((target, c), ((target - 1) % n_row, c - 1))]
        rest = {}
        for slot in range(ends):
            rest[slot] = block(
                pos, root_factor, rhs, col=c, slot=slot, rows=(0, own),
                columns=(0, own), sources=sources,
                bases=[] if last else [(shifted[slot], 0)], waits=(whole,),
            )
        if not last:
            solved = keep(pos, c, sources, rhs, solved, (whole,))
        if c > 1:
            early = move(upper, pair)
            late = move(lower, pair)
        others = {
            d: move(whole, [((target, c), ((target - d) % n_row, c - 1))])
            for d in range(2 if c > 1 else 1, n_row)
        }
        shifted = {
            slot: move(value, [((r, c), (r, c - 1)) for r in range(n_row)])
            for slot, value in [(ends, whole), *rest.items()]
        }
        if last:
            held, _ = lax.optimization_barrier((child_map, whole))
            asked = lax.all_to_all(
                held.reshape(n_col, per_front), "col", split_axis=0, concat_axis=0, tiled=True
            )
            asked = asked - col * own

    sources = [(0, ((shifted[0], 0, 0, own),))]
    sources += [(d, ((others[d], 0, 0, own),)) for d in range(1, n_row)]
    solved = keep(pos, 0, sources, rhs, solved, ())
    cases = tuple((c, None, None, n_row) for c in range(n_col))
    picks = [solved] * (n_col - 1) + [rhs]
    solved, served = serve(cases, pos, asked, picks)
    parents = lax.all_to_all(served, "col", split_axis=0, concat_axis=0, tiled=True)
    child = couple(parents, child_factor[0], child_rhs[0].T)
    return solved.T, child.T[None]


def body(root_factor, *rest):
    n_row, n_col = lax.axis_size("row"), lax.axis_size("col")
    if root_factor.shape[0] * n_row == n_col and n_row > 2:
        return chain_body(root_factor, *rest)
    return plain_body(root_factor, *rest)


def solution(mesh):
    return jax.shard_map(
        body,
        mesh=mesh,
        in_specs=(
            P(None, "row", None, "col"),
            P("col", None),
            P("col", "row", None),
            P("col", "row", None),
            P("col", None),
        ),
        out_specs=(P("col", None), P("col", "row", None)),
        check_vma=False,
    )
```
